32 devices in a mesh: row: 16 (over z, x, core), col: 2 (over y).
Axes of the slice: x: 2, y: 2, z: 4, core: 2. Of those that a mesh axis runs over, the one named last changes fastest.
Arguments:
- features: bfloat16 [4096, 256], P(('row', 'col')), may hold values from -6 to 6
- weight: bfloat16 [256, 256], replicated, may hold values from -0.375 to 0.375
- grad_out: bfloat16 [4096, 256], P(('row', 'col')), may hold values from -6 to 6
- tiles: bfloat16 [16, 2, 24, 128, 128], P('row', 'col'), may hold values from -0.109375 to 0.109375
- slots: int32 [16, 2, 24], P('row', 'col'), may hold values from 0 to 31, as said below
Outputs:
- activated: bfloat16 [4096, 256], P(('row', 'col'))
- grad_weight: float32 [256, 256], replicated
- grad_in: bfloat16 [4096, 256], P(('row', 'col'))
The draws below stay inside these ranges and needn't reach their ends.
Inputs may be any that keep to these rules, and one draw needn't show every extreme that they name: `slots`: within one tile the 24 entries are distinct.
All inputs are finite; a program needn't handle non-finite values.
Results may differ from the reference program's by a relative error of at most 0.0061.
Values may be sent and summed in bfloat16 or wider, within the bound.
No kernel may reach another device: no remote copies, remote signals or barrier semaphores. Data moves between devices by JAX's collectives and lax.ppermute only.
A program may use at most 128 MiB of HBM per device.

```python
import jax
import jax.numpy as jnp
from jax import lax

F = 256
BLK = 128
M = 128
NODES = 4096
ROW_BLOCKS = 2
COL_BLOCKS = 16
BLOCKS = 24
N_ROW = 16
N_COL = 2


def draw_slots(key, part):
    keys = jax.random.split(key, N_ROW * N_COL)

    def single(one_key):
        return jax.random.permutation(one_key, ROW_BLOCKS * COL_BLOCKS)[:BLOCKS].astype(jnp.int32)
    return jax.vmap(single)(keys).reshape(N_ROW, N_COL, BLOCKS)


def shard_levels(rng, dims, pieces, least, largest):
    level = 1.0
    for axis_at, shards_of in pieces:
        draws = jax.random.uniform(jax.random.fold_in(jax.random.fold_in(rng, 6), axis_at), (shards_of,), jnp.float32, least / len(pieces), largest / len(pieces))
        level = level * jnp.repeat(jnp.exp(draws), dims[axis_at] // shards_of).reshape((-1,) + (1,) * (len(dims) - 1 - axis_at))
    return level


def normal_values(stream_key, extent, spread, limit, pieces=(), held_as=jnp.bfloat16):
    level = shard_levels(stream_key, extent, pieces, -0.22, 0.18) if pieces else 1.0
    drawn = jax.random.normal(stream_key, extent, jnp.float32) * spread * level
    return jnp.minimum(jnp.maximum(drawn, -limit), limit).astype(held_as)


def setup_inputs(seed: int = 0) -> dict:
    key_list = jax.random.split(jax.random.key(seed), 6)
    return {
        "features": normal_values(key_list[0], (NODES, F), 1.0, 6.0, ((0, 32),)),
        "weight": normal_values(key_list[1], (F, F), F ** -0.5, 0.375),
        "grad_out": normal_values(key_list[2], (NODES, F), 1.0, 6.0, ((0, 32),)),
        "tiles": normal_values(key_list[3], (N_ROW, N_COL, BLOCKS, BLK, BLK), (BLOCKS * BLK * N_COL // ROW_BLOCKS) ** -0.5, 0.109375, ((0, 16), (1, 2))),
        "slots": draw_slots(jax.random.fold_in(key_list[5], 71), 0),
    }


def forward_tile(tile_blocks, tile_slots, column_panel):
    block_rows = tile_slots // COL_BLOCKS
    block_cols = tile_slots % COL_BLOCKS
    picked = column_panel[block_cols].astype(jnp.float32)
    products = jnp.einsum("kij,kjf->kif", tile_blocks.astype(jnp.float32), picked)
    return jax.ops.segment_sum(products, block_rows, num_segments=ROW_BLOCKS)


def backward_tile(tile_blocks, tile_slots, row_panel):
    block_rows = tile_slots // COL_BLOCKS
    block_cols = tile_slots % COL_BLOCKS
    picked = row_panel[block_rows].astype(jnp.float32)
    products = jnp.einsum("kji,kjf->kif", tile_blocks.astype(jnp.float32), picked)
    return jax.ops.segment_sum(products, block_cols, num_segments=COL_BLOCKS)


def reference(features, weight, grad_out, tiles, slots):
    shards = features.reshape(N_ROW, N_COL, M, F)

    def forward_step(totals, flat):
        row_index = flat // N_COL
        col_index = flat % N_COL
        column_panel = lax.dynamic_index_in_dim(shards, col_index, 1, keepdims=False).reshape(COL_BLOCKS, BLK, F)
        partial_sum = forward_tile(tiles[row_index, col_index], slots[row_index, col_index], column_panel)
        return totals.at[row_index].add(partial_sum.reshape(N_COL * M, F)), None

    flats = jnp.arange(N_ROW * N_COL, dtype=jnp.int32)
    totals, ignored = lax.scan(forward_step, jnp.zeros((N_ROW, N_COL * M, F), jnp.float32), flats)
    aggregated = totals.reshape(NODES, F).astype(jnp.bfloat16)
    pre = jnp.dot(aggregated, weight, preferred_element_type=jnp.float32)
    sigmoid_pre = jax.nn.sigmoid(pre)
    activated = (pre * sigmoid_pre).astype(jnp.bfloat16)
    grad_pre = (grad_out.astype(jnp.float32) * sigmoid_pre * (1.0 + pre * (1.0 - sigmoid_pre))).astype(jnp.bfloat16)
    grad_weight = jnp.dot(aggregated.T, grad_pre, preferred_element_type=jnp.float32) * (1.0 / NODES ** 0.5)
    grad_agg = jnp.dot(grad_pre, weight.T, preferred_element_type=jnp.float32).astype(jnp.bfloat16)
    row_panels = grad_agg.reshape(N_ROW, ROW_BLOCKS, BLK, F)

    def backward_step(totals_back, flat):
        row_index = flat // N_COL
        col_index = flat % N_COL
        partial_sum = backward_tile(tiles[row_index, col_index], slots[row_index, col_index], row_panels[row_index])
        return totals_back.at[col_index].add(partial_sum), None

    totals_back, ignored_back = lax.scan(backward_step, jnp.zeros((N_COL, COL_BLOCKS, BLK, F), jnp.float32), flats)
    grad_in = totals_back.reshape(N_COL, N_ROW, M, F).transpose(1, 0, 2, 3).reshape(NODES, F).astype(jnp.bfloat16)
    return activated, grad_weight, grad_in
```

```python
import math

import jax
import jax.numpy as jnp
from jax import lax
from jax.sharding import PartitionSpec as P


def swap(x, axis, bit):
    return lax.ppermute(x, axis, [(i, i ^ bit) for i in range(lax.axis_size(axis))])


def bits(count):
    return [1 << k for k in range(count.bit_length() - 1)]


def tree_sum(terms):
    while len(terms) > 1:
        terms = [a + b for a, b in zip(terms[::2], terms[1::2])]
    return terms[0]


def gather_panel(features, row_count):
    depth = row_count // 4
    panel = jnp.concatenate([features] + [swap(features, "row", 4 * k) for k in range(1, depth)])
    panel = jnp.concatenate([panel, swap(panel, "row", 2)])
    return jnp.concatenate([panel, swap(panel, "row", 1)])


def scatter_sum(dense, row_panel, row_count):
    depth = row_count // 4
    half = row_count // 2
    spec = "bpij,bif->pjf"
    theirs = jnp.einsum(spec, dense[:, half:], row_panel, preferred_element_type=jnp.float32)
    theirs = swap(theirs.astype(jnp.bfloat16), "row", 1)
    mine = jnp.einsum(spec, dense[:, :half], row_panel, preferred_element_type=jnp.float32)
    mine = mine + theirs
    mine = mine[:depth] + swap(mine[depth:].astype(jnp.bfloat16), "row", 2)
    sent = mine[1:].astype(jnp.bfloat16)
    got = [swap(sent[k - 1], "row", 4 * k) for k in range(1, depth)]
    return tree_sum([mine[0]] + [g.astype(jnp.float32) for g in got])


def total_sum(term, row, row_count, col_count):
    depth = row_count // 4
    rows = term.shape[0] // 2
    core = row % 2
    pair = term.reshape(2, rows, -1)
    half = lax.dynamic_index_in_dim(pair, core, 0, False) + swap(
        lax.dynamic_index_in_dim(pair, 1 - core, 0, False), "row", 1
    )
    for bit in bits(col_count):
        sent = half.astype(jnp.bfloat16)
        half = sent.astype(jnp.float32) + swap(sent, "col", bit).astype(jnp.float32)
    sent = half.astype(jnp.bfloat16)
    terms = [sent] + [swap(sent, "row", 4 * k) for k in range(1, depth)]
    half = tree_sum([t.astype(jnp.float32) for t in terms])
    sent = half.astype(jnp.bfloat16)
    half = sent.astype(jnp.float32) + swap(sent, "row", 2).astype(jnp.float32)
    other = swap(half, "row", 1)
    low = jnp.where(core == 0, half, other)
    high = jnp.where(core == 0, other, half)
    return jnp.concatenate([low, high])


def local(features, weight, grad_out, tiles, slots):
    tile_blocks = tiles[0, 0]
    tile_slots = slots[0, 0]
    own_rows, width = features.shape
    side = tile_blocks.shape[1]
    row_count = lax.axis_size("row")
    col_count = lax.axis_size("col")
    row = lax.axis_index("row")
    col = lax.axis_index("col")
    relative = (tile_slots % row_count) ^ row
    position = (relative % 2) * (row_count // 2) + (relative // 2 % 2) * (row_count // 4) + relative // 4
    position = ((tile_slots // row_count) ^ col) * row_count + position
    dense = (
        jnp.zeros((col_count * row_count, side, side), jnp.bfloat16).at[position].set(tile_blocks)
    )
    dense = dense.reshape(col_count, row_count, side, side)

    panel = gather_panel(features, row_count).reshape(row_count, side, width)
    partial = jnp.einsum("bpij,pjf->bif", dense, panel, preferred_element_type=jnp.float32)
    cotangent = grad_out[None]
    for bit in bits(col_count):
        cotangent = jnp.concatenate([cotangent, swap(cotangent, "col", bit)])
        got = swap(partial.astype(jnp.bfloat16), "col", bit)
        got = got.reshape(-1, 2, bit, side, width)[:, ::-1].reshape(partial.shape)
        partial = partial + got
    aggregated = partial.astype(jnp.bfloat16).reshape(-1, width)
    cotangent = cotangent.reshape(-1, width)
    pre = jnp.dot(aggregated, weight, preferred_element_type=jnp.float32)
    sigmoid_pre = jax.nn.sigmoid(pre)
    activated = (pre[:own_rows] * sigmoid_pre[:own_rows]).astype(jnp.bfloat16)
    grad_pre = (
        cotangent.astype(jnp.float32) * sigmoid_pre * (1.0 + pre * (1.0 - sigmoid_pre))
    ).astype(jnp.bfloat16)
    weight_term = jnp.dot(
        aggregated[:own_rows].T, grad_pre[:own_rows], preferred_element_type=jnp.float32
    )
    grad_agg = jnp.dot(grad_pre, weight.T, preferred_element_type=jnp.float32).astype(jnp.bfloat16)
    grad_in = scatter_sum(dense, grad_agg.reshape(col_count, side, width), row_count)
    total_nodes = own_rows * row_count * col_count
    grad_weight = total_sum(weight_term, row, row_count, col_count) * (1.0 / math.sqrt(total_nodes))
    return (activated, grad_weight, grad_in.astype(jnp.bfloat16))


def solution(mesh):
    in_specs = (
        P(("row", "col"), None),
        P(),
        P(("row", "col"), None),
        P("row", "col", None, None, None),
        P("row", "col", None),
    )
    out_specs = (P(("row", "col"), None), P(), P(("row", "col"), None))
    return jax.shard_map(local, mesh=mesh, in_specs=in_specs, out_specs=out_specs, check_vma=False)
```

```python
import math

import jax
import jax.numpy as jnp
from jax import lax
from jax.sharding import PartitionSpec as P


def swap(x, axis, bit):
    return lax.ppermute(x, axis, [(i, i ^ bit) for i in range(lax.axis_size(axis))])


def bits(count):
    return [1 << k for k in range(count.bit_length() - 1)]


def tree_sum(terms):
    while len(terms) > 1:
        terms = [a + b for a, b in zip(terms[::2], terms[1::2])]
    return terms[0]


def rounded(x):
    return lax.optimization_barrier(x.astype(jnp.bfloat16))


def local(features, weight, grad_out, tiles, slots):
    tile_blocks = tiles[0, 0]
    tile_slots = slots[0, 0]
    own_rows, width = features.shape
    side = tile_blocks.shape[1]
    row_count = lax.axis_size("row")
    col_count = lax.axis_size("col")
    row = lax.axis_index("row")
    col = lax.axis_index("col")
    core = row & 1
    depth = row_count // 4
    f32 = jnp.float32
    bf16 = jnp.bfloat16

    relative = (tile_slots % row_count) ^ row
    position = (relative % 2) * (row_count // 2) + (relative // 2 % 2) * depth + relative // 4
    position = tile_slots // row_count * row_count + position
    dense = jnp.zeros((col_count * row_count, side, side), bf16).at[position].set(tile_blocks)
    cotangent = grad_out
    for bit in bits(col_count):
        got = swap(cotangent, "col", bit)
        low = jnp.where(col & bit == 0, cotangent, got)
        high = jnp.where(col & bit == 0, got, cotangent)
        cotangent = jnp.concatenate([low, high])
    panel = jnp.concatenate([features] + [swap(features, "row", 4 * k) for k in range(1, depth)])
    panel, dense, cotangent = lax.optimization_barrier((panel, dense, cotangent))
    dense = dense.reshape(col_count, 4, depth, side, side)

    def forward(quarter, block):
        return jnp.einsum(
            "bpij,pjf->bif",
            dense[:, quarter],
            block.reshape(depth, side, width),
            preferred_element_type=f32,
        )

    def backward(quarter, row_panel):
        return jnp.einsum(
            "bpij,bif->pjf", dense[:, quarter], row_panel, preferred_element_type=f32
        )

    panel_x = swap(panel, "row", 2)
    panel_c = swap(panel, "row", 1)
    partial = forward(0, panel) + forward(2, panel_c)
    panel_xc = swap(panel_x, "row", 1)
    partial = partial + forward(1, panel_x) + forward(3, panel_xc)
    for bit in bits(col_count):
        sent = rounded(partial)
        partial = sent.astype(f32) + swap(sent, "col", bit).astype(f32)
    aggregated = partial.astype(bf16).reshape(-1, width)
    pre = jnp.dot(aggregated, weight, preferred_element_type=f32)
    sigmoid_pre = jax.nn.sigmoid(pre)
    grad_pre = (
        cotangent.astype(f32) * sigmoid_pre * (1.0 + pre * (1.0 - sigmoid_pre))
    ).astype(bf16)
    grad_agg = jnp.dot(grad_pre, weight.T, preferred_element_type=f32).astype(bf16)
    row_panel = grad_agg.reshape(col_count, side, width)

    sent_xc = backward(3, row_panel).astype(bf16)
    sent_xc, aggregated = lax.optimization_barrier((sent_xc, aggregated))
    got_xc = swap(sent_xc, "row", 1)
    term = jnp.dot(aggregated.T, grad_pre, preferred_element_type=f32)
    got_c = swap(backward(2, row_panel).astype(bf16), "row", 1)

    sent_x = (backward(1, row_panel) + got_xc.astype(f32)).astype(bf16)
    sent_x, term = lax.optimization_barrier((sent_x, term))
    got_x = swap(sent_x, "row", 2)
    mine = backward(0, row_panel) + got_c.astype(f32)

    pair = term.reshape(2, term.shape[0] // 2, -1)
    half = lax.dynamic_index_in_dim(pair, core, 0, False) + swap(
        lax.dynamic_index_in_dim(pair, 1 - core, 0, False), "row", 1
    )
    for bit in bits(depth):
        sent = rounded(half)
        half = sent.astype(f32) + swap(sent, "row", 4 * bit).astype(f32)

    mine = mine + got_x.astype(f32)
    sent_z = [mine[k].astype(bf16) for k in range(1, depth)]
    *sent_z, sent = lax.optimization_barrier((*sent_z, half.astype(bf16)))
    got_z = [swap(sent_z[k - 1], "row", 4 * k).astype(f32) for k in range(1, depth)]
    grad_in = tree_sum([mine[0]] + got_z)

    half = sent.astype(f32) + swap(sent, "row", 2).astype(f32)
    other = swap(half, "row", 1)
    low = jnp.where(core == 0, half, other)
    high = jnp.where(core == 0, other, half)
    total_nodes = own_rows * row_count * col_count
    grad_weight = jnp.concatenate([low, high]) * (1.0 / math.sqrt(total_nodes))

    start = col * own_rows
    own_pre = lax.dynamic_slice_in_dim(pre, start, own_rows)
    own_sigmoid = lax.dynamic_slice_in_dim(sigmoid_pre, start, own_rows)
    activated = (own_pre * own_sigmoid).astype(bf16)
    return (activated, grad_weight, grad_in.astype(bf16))


def solution(mesh):
    in_specs = (
        P(("row", "col"), None),
        P(),
        P(("row", "col"), None),
        P("row", "col", None, None, None),
        P("row", "col", None),
    )
    out_specs = (P(("row", "col"), None), P(), P(("row", "col"), None))
    return jax.shard_map(local, mesh=mesh, in_specs=in_specs, out_specs=out_specs, check_vma=False)
```

```python
import math

import jax
import jax.numpy as jnp
from jax import lax
from jax.experimental import pallas as pl
from jax.experimental.pallas import tpu as pltpu
from jax.sharding import PartitionSpec as P


def swap(x, axis, bit):
    return lax.ppermute(x, axis, [(i, i ^ bit) for i in range(lax.axis_size(axis))])


def bits(count):
    return [1 << k for k in range(count.bit_length() - 1)]


def total(terms, dtype, flops, later_than=()):
    count = len(terms)

    def body(*refs):
        value = refs[0][...].astype(jnp.float32)
        for ref in refs[1:count]:
            value = value + ref[...].astype(jnp.float32)
        refs[-1][...] = value.astype(dtype)

    shape = jax.ShapeDtypeStruct(terms[0].shape, dtype)
    in_specs = [pl.BlockSpec(memory_space=pltpu.VMEM)] * count
    in_specs += [pl.BlockSpec(memory_space=pl.ANY)] * len(later_than)
    return pl.pallas_call(
        body,
        out_shape=shape,
        in_specs=in_specs,
        out_specs=pl.BlockSpec(memory_space=pltpu.VMEM),
        compiler_params=pltpu.CompilerParams(vmem_limit_bytes=4 << 20),
        cost_estimate=pl.CostEstimate(flops=flops, bytes_accessed=4 * shape.size, transcendentals=0),
    )(*terms, *later_than)


def tree_sum(terms):
    while len(terms) > 1:
        terms = [a + b for a, b in zip(terms[::2], terms[1::2])]
    return terms[0]


def finish(terms, half, other, core, scale):
    count = len(terms)
    rows, width = half.shape

    def body(core_ref, *refs):
        half_ref, other_ref, grad_ref, weight_ref = refs[count:]
        value = refs[0][...]
        for ref in refs[1:count]:
            value = value + ref[...].astype(jnp.float32)
        grad_ref[...] = value.astype(jnp.bfloat16)
        first = pl.multiple_of(core_ref[0] * rows, rows)
        second = pl.multiple_of(rows - core_ref[0] * rows, rows)
        weight_ref[pl.ds(first, rows), :] = half_ref[...] * scale
        weight_ref[pl.ds(second, rows), :] = other_ref[...] * scale

    vmem = pl.BlockSpec(memory_space=pltpu.VMEM)
    return pl.pallas_call(
        body,
        out_shape=(
            jax.ShapeDtypeStruct(terms[0].shape, jnp.bfloat16),
            jax.ShapeDtypeStruct((2 * rows, width), jnp.float32),
        ),
        in_specs=[pl.BlockSpec(memory_space=pltpu.SMEM)] + [vmem] * (count + 2),
        out_specs=(vmem, vmem),
        compiler_params=pltpu.CompilerParams(vmem_limit_bytes=4 << 20),
        cost_estimate=pl.CostEstimate(flops=10**6, bytes_accessed=10**6, transcendentals=0),
    )(core.reshape(1), *terms, half, other)


def rounded(x):
    return lax.optimization_barrier(x.astype(jnp.bfloat16))


def local(features, weight, grad_out, tiles, slots):
    tile_blocks = tiles[0, 0]
    tile_slots = slots[0, 0]
    own_rows, width = features.shape
    side = tile_blocks.shape[1]
    row_count = lax.axis_size("row")
    col_count = lax.axis_size("col")
    row = lax.axis_index("row")
    col = lax.axis_index("col")
    core = row & 1
    depth = row_count // 4
    f32 = jnp.float32
    bf16 = jnp.bfloat16

    relative = (tile_slots % row_count) ^ row
    position = (relative % 2) * (row_count // 2) + (relative // 2 % 2) * depth + relative // 4
    position = tile_slots // row_count * row_count + position
    dense = jnp.zeros((col_count * row_count, side, side), bf16).at[position].set(tile_blocks)
    cotangent = grad_out
    for bit in bits(col_count):
        got = swap(cotangent, "col", bit)
        low = jnp.where(col & bit == 0, cotangent, got)
        high = jnp.where(col & bit == 0, got, cotangent)
        cotangent = jnp.concatenate([low, high])
    panel = jnp.concatenate([features] + [swap(features, "row", 4 * k) for k in range(1, depth)])
    panel, dense, cotangent = lax.optimization_barrier((panel, dense, cotangent))
    dense = dense.reshape(col_count, 4, depth, side, side)

    def forward(quarter, block):
        return jnp.einsum(
            "bpij,pjf->bif",
            dense[:, quarter],
            block.reshape(depth, side, width),
            preferred_element_type=f32,
        )

    def backward(quarter, row_panel):
        return jnp.einsum(
            "bpij,bif->pjf", dense[:, quarter], row_panel, preferred_element_type=f32
        )

    panel_x = swap(panel, "row", 2)
    panel_c = swap(panel, "row", 1)
    partial = forward(0, panel) + forward(2, panel_c)
    panel_xc = swap(panel_x, "row", 1)
    partial = partial + forward(1, panel_x) + forward(3, panel_xc)
    for bit in bits(col_count):
        sent = rounded(partial)
        partial = sent.astype(f32) + swap(sent, "col", bit).astype(f32)
    aggregated = partial.astype(bf16).reshape(-1, width)
    pre = jnp.dot(aggregated, weight, preferred_element_type=f32)
    sigmoid_pre = jax.nn.sigmoid(pre)
    grad_pre = (
        cotangent.astype(f32) * sigmoid_pre * (1.0 + pre * (1.0 - sigmoid_pre))
    ).astype(bf16)
    term = jnp.dot(aggregated.T, grad_pre, preferred_element_type=f32)
    grad_pre, term = lax.optimization_barrier((grad_pre, term))
    grad_agg = jnp.dot(grad_pre, weight.T, preferred_element_type=f32).astype(bf16)
    row_panel = grad_agg.reshape(col_count, side, width)

    sent_xc = backward(3, row_panel).astype(bf16)
    got_xc = swap(sent_xc, "row", 1)
    got_c = swap(backward(2, row_panel).astype(bf16), "row", 1)

    sent_x = (backward(1, row_panel) + got_xc.astype(f32)).astype(bf16)
    got_x = swap(sent_x, "row", 2)
    mine = backward(0, row_panel) + got_c.astype(f32)

    pair = term.reshape(2, term.shape[0] // 2, -1)
    kept = lax.dynamic_index_in_dim(pair, core, 0, False)
    got = swap(lax.dynamic_index_in_dim(pair, 1 - core, 0, False), "row", 1)
    half = total([kept, got], bf16, 3000000000, [sent_x])

    mine = mine + got_x.astype(f32)
    sent_z = [mine[k].astype(bf16) for k in range(1, depth)]
    for bit in bits(depth):
        last = [sent_z[-1]] if 2 * bit == depth else []
        half = total([half, swap(half, "row", 4 * bit)], bf16, 3000000000 if last else 100000000, last)
    got_z = [swap(sent_z[k - 1], "row", 4 * k) for k in range(1, depth)]
    half = total([half, swap(half, "row", 2)], f32, 10**8)
    total_nodes = own_rows * row_count * col_count
    scale = 1.0 / math.sqrt(total_nodes)
    grad_sum = total([mine[0]] + got_z, f32, 3 * 10**9)
    grad_in, grad_weight = finish([grad_sum], half, swap(half, "row", 1), core, scale)

    start = col * own_rows
    own_pre = lax.dynamic_slice_in_dim(pre, start, own_rows)
    own_sigmoid = lax.dynamic_slice_in_dim(sigmoid_pre, start, own_rows)
    activated = (own_pre * own_sigmoid).astype(bf16)
    return (activated, grad_weight, grad_in)


def solution(mesh):
    in_specs = (
        P(("row", "col"), None),
        P(),
        P(("row", "col"), None),
        P("row", "col", None, None, None),
        P("row", "col", None),
    )
    out_specs = (P(("row", "col"), None), P(), P(("row", "col"), None))
    return jax.shard_map(local, mesh=mesh, in_specs=in_specs, out_specs=out_specs, check_vma=False)
```

```python
import math

import jax
import jax.numpy as jnp
from jax import lax
from jax.experimental import pallas as pl
from jax.experimental.pallas import tpu as pltpu
from jax.sharding import PartitionSpec as P


def swap(x, axis, bit):
    return lax.ppermute(x, axis, [(i, i ^ bit) for i in range(lax.axis_size(axis))])


def bits(count):
    return [1 << k for k in range(count.bit_length() - 1)]


def total(terms, dtype, flops, later_than=()):
    count = len(terms)

    def body(*refs):
        value = refs[0][...].astype(jnp.float32)
        for ref in refs[1:count]:
            value = value + ref[...].astype(jnp.float32)
        refs[-1][...] = value.astype(dtype)

    shape = jax.ShapeDtypeStruct(terms[0].shape, dtype)
    in_specs = [pl.BlockSpec(memory_space=pltpu.VMEM)] * count
    in_specs += [pl.BlockSpec(memory_space=pl.ANY)] * len(later_than)
    return pl.pallas_call(
        body,
        out_shape=shape,
        in_specs=in_specs,
        out_specs=pl.BlockSpec(memory_space=pltpu.VMEM),
        compiler_params=pltpu.CompilerParams(vmem_limit_bytes=4 << 20),
        cost_estimate=pl.CostEstimate(flops=flops, bytes_accessed=4 * shape.size, transcendentals=0),
    )(*terms, *later_than)


def tree_sum(terms):
    while len(terms) > 1:
        terms = [a + b for a, b in zip(terms[::2], terms[1::2])]
    return terms[0]


def finish(terms, half, other, core, scale):
    count = len(terms)
    rows, width = half.shape

    def body(core_ref, *refs):
        half_ref, other_ref, grad_ref, weight_ref = refs[count:]
        value = refs[0][...]
        for ref in refs[1:count]:
            value = value + ref[...].astype(jnp.float32)
        grad_ref[...] = value.astype(jnp.bfloat16)
        first = pl.multiple_of(core_ref[0] * rows, rows)
        second = pl.multiple_of(rows - core_ref[0] * rows, rows)
        weight_ref[pl.ds(first, rows), :] = half_ref[...] * scale
        weight_ref[pl.ds(second, rows), :] = other_ref[...] * scale

    vmem = pl.BlockSpec(memory_space=pltpu.VMEM)
    return pl.pallas_call(
        body,
        out_shape=(
            jax.ShapeDtypeStruct(terms[0].shape, jnp.bfloat16),
            jax.ShapeDtypeStruct((2 * rows, width), jnp.float32),
        ),
        in_specs=[pl.BlockSpec(memory_space=pltpu.SMEM)] + [vmem] * (count + 2),
        out_specs=(vmem, vmem),
        compiler_params=pltpu.CompilerParams(vmem_limit_bytes=4 << 20),
        cost_estimate=pl.CostEstimate(flops=10**6, bytes_accessed=10**6, transcendentals=0),
    )(core.reshape(1), *terms, half, other)


def dense_tile(tiles, slots, row, col, row_count, col_count, flops, later_than):
    blocks, side, _ = tiles.shape
    depth = row_count // 4

    def body(slots_ref, row_ref, tiles_ref, *refs):
        out_ref = refs[-1]
        out_ref[...] = jnp.zeros_like(out_ref)

        @pl.loop(0, blocks)
        def _(k):
            slot = slots_ref[k]
            relative = (slot & (row_count - 1)) ^ row_ref[0]
            place = (relative & 1) * (row_count // 2) + (relative >> 1 & 1) * depth
            place = place + (relative >> 2) + (slot - (slot & (row_count - 1)))
            out_ref[place] = tiles_ref[k]

    shape = jax.ShapeDtypeStruct((col_count * row_count, side, side), tiles.dtype)
    smem = pl.BlockSpec(memory_space=pltpu.SMEM)
    vmem = pl.BlockSpec(memory_space=pltpu.VMEM)
    return pl.pallas_call(
        body,
        out_shape=shape,
        in_specs=[smem, smem, vmem] + [pl.BlockSpec(memory_space=pl.ANY)] * len(later_than),
        out_specs=vmem,
        compiler_params=pltpu.CompilerParams(vmem_limit_bytes=(2 * (blocks + row_count * col_count) * side * side * 2) + (1 << 20)),
        cost_estimate=pl.CostEstimate(flops=flops, bytes_accessed=10**6, transcendentals=0),
    )(slots, row.reshape(1), tiles, *later_than)


def rounded(x):
    return lax.optimization_barrier(x.astype(jnp.bfloat16))


def local(features, weight, grad_out, tiles, slots):
    tile_blocks = tiles[0, 0]
    tile_slots = slots[0, 0]
    own_rows, width = features.shape
    side = tile_blocks.shape[1]
    row_count = lax.axis_size("row")
    col_count = lax.axis_size("col")
    row = lax.axis_index("row")
    col = lax.axis_index("col")
    core = row & 1
    depth = row_count // 4
    f32 = jnp.float32
    bf16 = jnp.bfloat16

    def direct(bit, low, high):
        return [swap(features, "row", 4 * k + bit) if k or bit else features for k in range(low, high)]

    straight = 1
    far = jnp.concatenate(direct(0, straight, depth))
    near = direct(0, 0, straight)
    near_x = jnp.concatenate(direct(2, 0, straight))
    panel = jnp.concatenate(near + [far])
    far_x = swap(far, "row", 2)

    cotangent = grad_out
    for bit in bits(col_count):
        got = swap(cotangent, "col", bit)
        low = jnp.where(col & bit == 0, cotangent, got)
        high = jnp.where(col & bit == 0, got, cotangent)
        cotangent = jnp.concatenate([low, high])
    dense = dense_tile(tile_blocks, tile_slots, row, col, row_count, col_count, 3000000000, [far])
    dense = dense.reshape(col_count, 4, depth, side, side)

    def forward(quarter, block):
        return jnp.einsum(
            "bpij,pjf->bif",
            dense[:, quarter],
            block.reshape(depth, side, width),
            preferred_element_type=f32,
        )

    def backward(quarter, row_panel):
        return jnp.einsum(
            "bpij,bif->pjf", dense[:, quarter], row_panel, preferred_element_type=f32
        )

    panel_c = swap(panel, "row", 1)
    near_xc = swap(near_x, "row", 1)
    partial = forward(0, panel) + forward(2, panel_c)
    far_x, cotangent, partial = lax.optimization_barrier((far_x, cotangent, partial))
    far_xc = swap(far_x, "row", 1)
    partial = partial + forward(1, jnp.concatenate([near_x, far_x]))
    partial = partial + forward(3, jnp.concatenate([near_xc, far_xc]))
    for bit in bits(col_count):
        sent = rounded(partial)
        partial = sent.astype(f32) + swap(sent, "col", bit).astype(f32)
    aggregated = partial.astype(bf16).reshape(-1, width)
    pre = jnp.dot(aggregated, weight, preferred_element_type=f32)
    sigmoid_pre = jax.nn.sigmoid(pre)
    grad_pre = (
        cotangent.astype(f32) * sigmoid_pre * (1.0 + pre * (1.0 - sigmoid_pre))
    ).astype(bf16)
    term = jnp.dot(aggregated.T, grad_pre, preferred_element_type=f32)
    grad_pre, term = lax.optimization_barrier((grad_pre, term))
    grad_agg = jnp.dot(grad_pre, weight.T, preferred_element_type=f32).astype(bf16)
    row_panel = grad_agg.reshape(col_count, side, width)

    sent_xc = backward(3, row_panel).astype(bf16)
    got_xc = swap(sent_xc, "row", 1)
    got_c = swap(backward(2, row_panel).astype(bf16), "row", 1)

    sent_x = (backward(1, row_panel) + got_xc.astype(f32)).astype(bf16)
    got_x = swap(sent_x, "row", 2)
    mine = backward(0, row_panel) + got_c.astype(f32)

    pair = term.reshape(2, term.shape[0] // 2, -1)
    kept = lax.dynamic_index_in_dim(pair, core, 0, False)
    got = swap(lax.dynamic_index_in_dim(pair, 1 - core, 0, False), "row", 1)
    half = total([kept, got], bf16, 3000000000, [sent_x])

    mine = mine + got_x.astype(f32)
    sent_z = [mine[k].astype(bf16) for k in range(1, depth)]
    for bit in bits(depth):
        last = [sent_z[-1]] if 2 * bit == depth else []
        half = total([half, swap(half, "row", 4 * bit)], bf16, 3000000000 if last else 100000000, last)
    got_z = [swap(sent_z[k - 1], "row", 4 * k) for k in range(1, depth)]
    half = total([half, swap(half, "row", 2)], f32, 10**8)
    total_nodes = own_rows * row_count * col_count
    scale = 1.0 / math.sqrt(total_nodes)
    grad_sum = total([mine[0]] + got_z, f32, 3 * 10**9)
    grad_in, grad_weight = finish([grad_sum], half, swap(half, "row", 1), core, scale)

    start = col * own_rows
    own_pre = lax.dynamic_slice_in_dim(pre, start, own_rows)
    own_sigmoid = lax.dynamic_slice_in_dim(sigmoid_pre, start, own_rows)
    activated = (own_pre * own_sigmoid).astype(bf16)
    return (activated, grad_weight, grad_in)


def solution(mesh):
    in_specs = (
        P(("row", "col"), None),
        P(),
        P(("row", "col"), None),
        P("row", "col", None, None, None),
        P("row", "col", None),
    )
    out_specs = (P(("row", "col"), None), P(), P(("row", "col"), None))
    return jax.shard_map(local, mesh=mesh, in_specs=in_specs, out_specs=out_specs, check_vma=False)
```

```python
import math

import jax
import jax.numpy as jnp
from jax import lax
from jax.experimental import pallas as pl
from jax.experimental.pallas import tpu as pltpu
from jax.sharding import PartitionSpec as P


def swap(x, axis, bit):
    return lax.ppermute(x, axis, [(i, i ^ bit) for i in range(lax.axis_size(axis))])


def bits(count):
    return [1 << k for k in range(count.bit_length() - 1)]


def total(terms, dtype, flops, later_than=()):
    count = len(terms)

    def body(*refs):
        value = refs[0][...].astype(jnp.float32)
        for ref in refs[1:count]:
            value = value + ref[...].astype(jnp.float32)
        refs[-1][...] = value.astype(dtype)

    shape = jax.ShapeDtypeStruct(terms[0].shape, dtype)
    in_specs = [pl.BlockSpec(memory_space=pltpu.VMEM)] * count
    in_specs += [pl.BlockSpec(memory_space=pl.ANY)] * len(later_than)
    return pl.pallas_call(
        body,
        out_shape=shape,
        in_specs=in_specs,
        out_specs=pl.BlockSpec(memory_space=pltpu.VMEM),
        compiler_params=pltpu.CompilerParams(vmem_limit_bytes=4 << 20),
        cost_estimate=pl.CostEstimate(flops=flops, bytes_accessed=4 * shape.size, transcendentals=0),
    )(*terms, *later_than)


def tree_sum(terms):
    while len(terms) > 1:
        terms = [a + b for a, b in zip(terms[::2], terms[1::2])]
    return terms[0]


def finish(terms, half, other, core, scale):
    count = len(terms)
    rows, width = half.shape

    def body(core_ref, *refs):
        half_ref, other_ref, grad_ref, weight_ref = refs[count:]
        value = refs[0][...]
        for ref in refs[1:count]:
            value = value + ref[...].astype(jnp.float32)
        grad_ref[...] = value.astype(jnp.bfloat16)
        first = pl.multiple_of(core_ref[0] * rows, rows)
        second = pl.multiple_of(rows - core_ref[0] * rows, rows)
        weight_ref[pl.ds(first, rows), :] = half_ref[...] * scale
        weight_ref[pl.ds(second, rows), :] = other_ref[...] * scale

    vmem = pl.BlockSpec(memory_space=pltpu.VMEM)
    return pl.pallas_call(
        body,
        out_shape=(
            jax.ShapeDtypeStruct(terms[0].shape, jnp.bfloat16),
            jax.ShapeDtypeStruct((2 * rows, width), jnp.float32),
        ),
        in_specs=[pl.BlockSpec(memory_space=pltpu.SMEM)] + [vmem] * (count + 2),
        out_specs=(vmem, vmem),
        compiler_params=pltpu.CompilerParams(vmem_limit_bytes=4 << 20),
        cost_estimate=pl.CostEstimate(flops=10**6, bytes_accessed=10**6, transcendentals=0),
    )(core.reshape(1), *terms, half, other)


def dense_tile(tiles, slots, row, col, row_count, col_count, flops, later_than):
    blocks, side, _ = tiles.shape
    depth = row_count // 4

    def body(slots_ref, row_ref, tiles_ref, *refs):
        out_ref = refs[-1]
        out_ref[...] = jnp.zeros_like(out_ref)

        @pl.loop(0, blocks)
        def _(k):
            slot = slots_ref[k]
            relative = (slot & (row_count - 1)) ^ row_ref[0]
            place = (relative & 1) * (row_count // 2) + (relative >> 1 & 1) * depth
            place = place + (relative >> 2) + (slot - (slot & (row_count - 1)))
            out_ref[place] = tiles_ref[k]

    shape = jax.ShapeDtypeStruct((col_count * row_count, side, side), tiles.dtype)
    smem = pl.BlockSpec(memory_space=pltpu.SMEM)
    vmem = pl.BlockSpec(memory_space=pltpu.VMEM)
    return pl.pallas_call(
        body,
        out_shape=shape,
        in_specs=[smem, smem, vmem] + [pl.BlockSpec(memory_space=pl.ANY)] * len(later_than),
        out_specs=vmem,
        compiler_params=pltpu.CompilerParams(vmem_limit_bytes=(2 * (blocks + row_count * col_count) * side * side * 2) + (1 << 20)),
        cost_estimate=pl.CostEstimate(flops=flops, bytes_accessed=10**6, transcendentals=0),
    )(slots, row.reshape(1), tiles, *later_than)


def rounded(x):
    return lax.optimization_barrier(x.astype(jnp.bfloat16))


def local(features, weight, grad_out, tiles, slots):
    tile_blocks = tiles[0, 0]
    tile_slots = slots[0, 0]
    own_rows, width = features.shape
    side = tile_blocks.shape[1]
    row_count = lax.axis_size("row")
    col_count = lax.axis_size("col")
    row = lax.axis_index("row")
    col = lax.axis_index("col")
    core = row & 1
    depth = row_count // 4
    f32 = jnp.float32
    bf16 = jnp.bfloat16

    def direct(bit, low, high):
        return [swap(features, "row", 4 * k + bit) if k or bit else features for k in range(low, high)]

    straight = 1
    far = jnp.concatenate(direct(0, straight, depth))
    near = direct(0, 0, straight)
    near_x = jnp.concatenate(direct(2, 0, straight))
    panel = jnp.concatenate(near + [far])
    far_x = swap(far, "row", 2)

    cotangent = grad_out
    for bit in bits(col_count):
        got = swap(cotangent, "col", bit)
        low = jnp.where(col & bit == 0, cotangent, got)
        high = jnp.where(col & bit == 0, got, cotangent)
        cotangent = jnp.concatenate([low, high])
    dense = dense_tile(tile_blocks, tile_slots, row, col, row_count, col_count, 3000000000, [far])
    dense = dense.reshape(col_count, 4, depth, side, side)

    def forward(quarter, block):
        return jnp.einsum(
            "bpij,pjf->bif",
            dense[:, quarter],
            block.reshape(depth, side, width),
            preferred_element_type=f32,
        )

    def backward(quarter, row_panel):
        return jnp.einsum(
            "bpij,bif->pjf", dense[:, quarter], row_panel, preferred_element_type=f32
        )

    panel_c = swap(panel, "row", 1)
    near_xc = swap(near_x, "row", 1)
    partial = forward(0, panel) + forward(2, panel_c)
    far_x, cotangent, partial = lax.optimization_barrier((far_x, cotangent, partial))
    far_xc = swap(far_x, "row", 1)
    partial = partial + forward(1, jnp.concatenate([near_x, far_x]))
    partial = partial + forward(3, jnp.concatenate([near_xc, far_xc]))
    for bit in bits(col_count):
        sent = rounded(partial)
        partial = sent.astype(f32) + swap(sent, "col", bit).astype(f32)
    aggregated = partial.astype(bf16).reshape(-1, width)
    pre = jnp.dot(aggregated, weight, preferred_element_type=f32)
    sigmoid_pre = jax.nn.sigmoid(pre)
    grad_pre = (
        cotangent.astype(f32) * sigmoid_pre * (1.0 + pre * (1.0 - sigmoid_pre))
    ).astype(bf16)
    term = jnp.dot(aggregated.T, grad_pre, preferred_element_type=f32)
    grad_pre, term = lax.optimization_barrier((grad_pre, term))
    grad_agg = jnp.dot(grad_pre, weight.T, preferred_element_type=f32).astype(bf16)
    row_panel = grad_agg.reshape(col_count, side, width)

    sent_xc = backward(3, row_panel).astype(bf16)
    got_xc = swap(sent_xc, "row", 1)
    got_c = swap(backward(2, row_panel).astype(bf16), "row", 1)

    sent_x = (backward(1, row_panel) + got_xc.astype(f32)).astype(bf16)
    got_x = swap(sent_x, "row", 2)
    mine = backward(0, row_panel) + got_c.astype(f32)

    pair = term.reshape(2, term.shape[0] // 2, -1)
    kept = lax.dynamic_index_in_dim(pair, core, 0, False)
    got = swap(lax.dynamic_index_in_dim(pair, 1 - core, 0, False), "row", 1)
    half = total([kept, got], bf16, 3000000000, [sent_x])

    mine = mine + got_x.astype(f32)
    sent_z = [mine[k].astype(bf16) for k in range(1, depth)]
    for bit in bits(depth):
        last = [sent_z[-1]] if 2 * bit == depth else []
        half = total([half, swap(half, "row", 4 * bit)], bf16, 3000000000 if last else 100000000, last)
    for k in (1,2,):
        sent_z[k - 1] = total([sent_z[k - 1]], bf16, 100000000, [half])
    got_z = [swap(sent_z[k - 1], "row", 4 * k) for k in range(1, depth)]
    half = total([half, swap(half, "row", 2)], f32, 10**8)
    total_nodes = own_rows * row_count * col_count
    scale = 1.0 / math.sqrt(total_nodes)
    grad_sum = total([mine[0]] + got_z, f32, 3 * 10**9)
    grad_in, grad_weight = finish([grad_sum], half, swap(half, "row", 1), core, scale)

    start = col * own_rows
    own_pre = lax.dynamic_slice_in_dim(pre, start, own_rows)
    own_sigmoid = lax.dynamic_slice_in_dim(sigmoid_pre, start, own_rows)
    activated = (own_pre * own_sigmoid).astype(bf16)
    return (activated, grad_weight, grad_in)


def solution(mesh):
    in_specs = (
        P(("row", "col"), None),
        P(),
        P(("row", "col"), None),
        P("row", "col", None, None, None),
        P("row", "col", None),
    )
    out_specs = (P(("row", "col"), None), P(), P(("row", "col"), None))
    return jax.shard_map(local, mesh=mesh, in_specs=in_specs, out_specs=out_specs, check_vma=False)
```

```python
import math

import jax
import jax.numpy as jnp
from jax import lax
from jax.experimental import pallas as pl
from jax.experimental.pallas import tpu as pltpu
from jax.sharding import PartitionSpec as P


def swap(x, axis, bit):
    return lax.ppermute(x, axis, [(i, i ^ bit) for i in range(lax.axis_size(axis))])


def bits(count):
    return [1 << k for k in range(count.bit_length() - 1)]


def total(terms, dtype, flops, later_than=()):
    count = len(terms)

    def body(*refs):
        values = [ref[...].astype(jnp.float32) for ref in refs[:count]]
        while len(values) > 1:
            values = [a + b for a, b in zip(values[::2], values[1::2])]
        refs[-1][...] = values[0].astype(dtype)

    shape = jax.ShapeDtypeStruct(terms[0].shape, dtype)
    in_specs = [pl.BlockSpec(memory_space=pltpu.VMEM)] * count
    in_specs += [pl.BlockSpec(memory_space=pl.ANY)] * len(later_than)
    return pl.pallas_call(
        body,
        out_shape=shape,
        in_specs=in_specs,
        out_specs=pl.BlockSpec(memory_space=pltpu.VMEM),
        compiler_params=pltpu.CompilerParams(vmem_limit_bytes=4 << 20),
        cost_estimate=pl.CostEstimate(flops=flops, bytes_accessed=4 * shape.size, transcendentals=0),
    )(*terms, *later_than)


def tree_sum(terms):
    while len(terms) > 1:
        terms = [a + b for a, b in zip(terms[::2], terms[1::2])]
    return terms[0]


def finish(terms, half, other, core, scale):
    count = len(terms)
    rows, width = half.shape

    def body(core_ref, *refs):
        half_ref, other_ref, grad_ref, weight_ref = refs[count:]
        value = refs[0][...]
        for ref in refs[1:count]:
            value = value + ref[...].astype(jnp.float32)
        grad_ref[...] = value.astype(jnp.bfloat16)
        first = pl.multiple_of(core_ref[0] * rows, rows)
        second = pl.multiple_of(rows - core_ref[0] * rows, rows)
        weight_ref[pl.ds(first, rows), :] = half_ref[...] * scale
        weight_ref[pl.ds(second, rows), :] = other_ref[...] * scale

    vmem = pl.BlockSpec(memory_space=pltpu.VMEM)
    return pl.pallas_call(
        body,
        out_shape=(
            jax.ShapeDtypeStruct(terms[0].shape, jnp.bfloat16),
            jax.ShapeDtypeStruct((2 * rows, width), jnp.float32),
        ),
        in_specs=[pl.BlockSpec(memory_space=pltpu.SMEM)] + [vmem] * (count + 2),
        out_specs=(vmem, vmem),
        compiler_params=pltpu.CompilerParams(vmem_limit_bytes=4 << 20),
        cost_estimate=pl.CostEstimate(flops=10**6, bytes_accessed=10**6, transcendentals=0),
    )(core.reshape(1), *terms, half, other)


def dense_tile(tiles, slots, row, col, row_count, col_count, flops, later_than):
    blocks, side, _ = tiles.shape
    depth = row_count // 4

    def body(slots_ref, row_ref, tiles_ref, *refs):
        own_ref, other_ref = refs[-2:]
        own_ref[...] = jnp.zeros_like(own_ref)
        other_ref[...] = jnp.zeros_like(other_ref)

        @pl.loop(0, blocks)
        def _(k):
            slot = slots_ref[k]
            relative = (slot & (row_count - 1)) ^ row_ref[0]
            place = (relative >> 1 & 1) * depth + (relative >> 2)
            place = place + (slot - (slot & (row_count - 1))) // 2

            @pl.when(relative & 1 == 0)
            def _():
                own_ref[place] = tiles_ref[k]

            @pl.when(relative & 1 == 1)
            def _():
                other_ref[place] = tiles_ref[k]

    shape = jax.ShapeDtypeStruct((col_count * row_count // 2, side, side), tiles.dtype)
    smem = pl.BlockSpec(memory_space=pltpu.SMEM)
    vmem = pl.BlockSpec(memory_space=pltpu.VMEM)
    return pl.pallas_call(
        body,
        out_shape=(shape, shape),
        in_specs=[smem, smem, vmem] + [pl.BlockSpec(memory_space=pl.ANY)] * len(later_than),
        out_specs=(vmem, vmem),
        compiler_params=pltpu.CompilerParams(vmem_limit_bytes=(2 * (blocks + row_count * col_count) * side * side * 2) + (1 << 20)),
        cost_estimate=pl.CostEstimate(flops=flops, bytes_accessed=10**6, transcendentals=0),
    )(slots, row.reshape(1), tiles, *later_than)


def rounded(x):
    return lax.optimization_barrier(x.astype(jnp.bfloat16))


def local(features, weight, grad_out, tiles, slots):
    tile_blocks = tiles[0, 0]
    tile_slots = slots[0, 0]
    own_rows, width = features.shape
    side = tile_blocks.shape[1]
    row_count = lax.axis_size("row")
    col_count = lax.axis_size("col")
    row = lax.axis_index("row")
    col = lax.axis_index("col")
    core = row & 1
    depth = row_count // 4
    f32 = jnp.float32
    bf16 = jnp.bfloat16

    def direct(bit, low, high):
        return [swap(features, "row", 4 * k + bit) if k or bit else features for k in reversed(range(low, high))][::-1]

    straight = 1
    far = jnp.concatenate(direct(0, straight, depth))
    near = direct(0, 0, straight)
    near_x = jnp.concatenate(direct(2, 0, straight))
    panel = jnp.concatenate(near + [far])
    far_x = swap(far, "row", 2)

    cotangent = grad_out
    for bit in bits(col_count):
        got = swap(cotangent, "col", bit)
        low = jnp.where(col & bit == 0, cotangent, got)
        high = jnp.where(col & bit == 0, got, cotangent)
        cotangent = jnp.concatenate([low, high])
    own_tile, other_tile = dense_tile(tile_blocks, tile_slots, row, col, row_count, col_count, 3000000000, [far])
    own_tile = own_tile.reshape(col_count, 2, depth, side, side)
    other_tile = other_tile.reshape(col_count, 2, depth, side, side)

    def forward(quarter, block):
        return jnp.einsum(
            "bpij,pjf->bif",
            (own_tile if quarter < 2 else other_tile)[:, quarter % 2],
            block.reshape(depth, side, width),
            preferred_element_type=f32,
        )

    panel_c = swap(panel, "row", 1)
    partial = forward(0, panel) + forward(2, panel_c)
    far_x, cotangent, partial = lax.optimization_barrier((far_x, cotangent, partial))
    panel_x = jnp.concatenate([near_x, far_x])
    partial = partial + forward(1, panel_x) + forward(3, swap(panel_x, "row", 1))
    for bit in bits(col_count):
        sent, other_tile = lax.optimization_barrier((partial.astype(bf16), other_tile))
        got = swap(sent, "col", bit)
        partial = sent.astype(f32) + got.astype(f32)
    partner = swap(other_tile, "row", 1)
    aggregated = partial.astype(bf16).reshape(-1, width)
    pre = jnp.dot(aggregated, weight, preferred_element_type=f32)
    sigmoid_pre = jax.nn.sigmoid(pre)
    grad_pre = (
        cotangent.astype(f32) * sigmoid_pre * (1.0 + pre * (1.0 - sigmoid_pre))
    ).astype(bf16)
    partner_grad_pre = swap(grad_pre, "row", 1)
    partner_aggregated = swap(aggregated, "row", 1)

    def panel_of(rows):
        grad_agg = jnp.dot(rows, weight.T, preferred_element_type=f32).astype(bf16)
        return grad_agg.reshape(col_count, side, width)

    row_panel = panel_of(grad_pre)
    partner_panel = panel_of(partner_grad_pre)

    def backward(quarter):
        spec = "bpij,bif->pjf"
        own = jnp.einsum(spec, own_tile[:, quarter], row_panel, preferred_element_type=f32)
        return own + jnp.einsum(spec, partner[:, quarter], partner_panel, preferred_element_type=f32)

    sent_x = backward(1).astype(bf16)
    sent_x, pre = lax.optimization_barrier((sent_x, pre))
    got_x = swap(sent_x, "row", 2)
    mine = backward(0)

    columns = [
        lax.dynamic_slice_in_dim(rows, core * (width // 2), width // 2, 1)
        for rows in (aggregated, partner_aggregated)
    ]
    half = jnp.dot(columns[0].T, grad_pre, preferred_element_type=f32)
    half = half + jnp.dot(columns[1].T, partner_grad_pre, preferred_element_type=f32)
    half = total([half], bf16, 3000000000, [sent_x])

    mine = mine + got_x.astype(f32)
    sent_z = [mine[k].astype(bf16) for k in range(1, depth)]
    half = total([half] + [swap(half, "row", 4 * k) for k in range(1, depth)], bf16, 3 * 10**9, [sent_z[-1]])
    for k in (1,):
        sent_z[k - 1] = total([sent_z[k - 1]], bf16, 100000000, [half])
    got_z = [swap(sent_z[k - 1], "row", 4 * k) for k in range(1, depth)]
    half = total([half, swap(half, "row", 2)], f32, 10**8)
    total_nodes = own_rows * row_count * col_count
    scale = 1.0 / math.sqrt(total_nodes)
    grad_sum = total([mine[0]] + got_z, f32, 3 * 10**9)
    grad_in, grad_weight = finish([grad_sum], half, swap(half, "row", 1), core, scale)

    start = col * own_rows
    own_pre = lax.dynamic_slice_in_dim(pre, start, own_rows)
    own_sigmoid = lax.dynamic_slice_in_dim(sigmoid_pre, start, own_rows)
    activated = (own_pre * own_sigmoid).astype(bf16)
    return (activated, grad_weight, grad_in)


def solution(mesh):
    in_specs = (
        P(("row", "col"), None),
        P(),
        P(("row", "col"), None),
        P("row", "col", None, None, None),
        P("row", "col", None),
    )
    out_specs = (P(("row", "col"), None), P(), P(("row", "col"), None))
    return jax.shard_map(local, mesh=mesh, in_specs=in_specs, out_specs=out_specs, check_vma=False)
```

```python
import math

import jax
import jax.numpy as jnp
from jax import lax
from jax.experimental import pallas as pl
from jax.experimental.pallas import tpu as pltpu
from jax.sharding import PartitionSpec as P


def swap(x, axis, bit):
    return lax.ppermute(x, axis, [(i, i ^ bit) for i in range(lax.axis_size(axis))])


def bits(count):
    return [1 << k for k in range(count.bit_length() - 1)]


def total(terms, dtype, flops, later_than=()):
    count = len(terms)

    def body(*refs):
        values = [ref[...].astype(jnp.float32) for ref in refs[:count]]
        while len(values) > 1:
            values = [a + b for a, b in zip(values[::2], values[1::2])]
        refs[-1][...] = values[0].astype(dtype)

    shape = jax.ShapeDtypeStruct(terms[0].shape, dtype)
    in_specs = [pl.BlockSpec(memory_space=pltpu.VMEM)] * count
    in_specs += [pl.BlockSpec(memory_space=pl.ANY)] * len(later_than)
    return pl.pallas_call(
        body,
        out_shape=shape,
        in_specs=in_specs,
        out_specs=pl.BlockSpec(memory_space=pltpu.VMEM),
        compiler_params=pltpu.CompilerParams(vmem_limit_bytes=4 << 20),
        cost_estimate=pl.CostEstimate(flops=flops, bytes_accessed=4 * shape.size, transcendentals=0),
    )(*terms, *later_than)


def tree_sum(terms):
    while len(terms) > 1:
        terms = [a + b for a, b in zip(terms[::2], terms[1::2])]
    return terms[0]


def finish(terms, half, other, core, scale):
    count = len(terms)
    rows, width = half.shape

    def body(core_ref, *refs):
        half_ref, other_ref, grad_ref, weight_ref = refs[count:]
        value = refs[0][...]
        for ref in refs[1:count]:
            value = value + ref[...].astype(jnp.float32)
        grad_ref[...] = value.astype(jnp.bfloat16)
        first = pl.multiple_of(core_ref[0] * rows, rows)
        second = pl.multiple_of(rows - core_ref[0] * rows, rows)
        weight_ref[pl.ds(first, rows), :] = half_ref[...] * scale
        weight_ref[pl.ds(second, rows), :] = other_ref[...] * scale

    vmem = pl.BlockSpec(memory_space=pltpu.VMEM)
    return pl.pallas_call(
        body,
        out_shape=(
            jax.ShapeDtypeStruct(terms[0].shape, jnp.bfloat16),
            jax.ShapeDtypeStruct((2 * rows, width), jnp.float32),
        ),
        in_specs=[pl.BlockSpec(memory_space=pltpu.SMEM)] + [vmem] * (count + 2),
        out_specs=(vmem, vmem),
        compiler_params=pltpu.CompilerParams(vmem_limit_bytes=4 << 20),
        cost_estimate=pl.CostEstimate(flops=10**6, bytes_accessed=10**6, transcendentals=0),
    )(core.reshape(1), *terms, half, other)


def dense_tile(tiles, slots, row, col, row_count, col_count, flops, later_than):
    blocks, side, _ = tiles.shape
    depth = row_count // 4

    def body(slots_ref, row_ref, tiles_ref, *refs):
        own_ref, other_ref = refs[-2:]
        own_ref[...] = jnp.zeros_like(own_ref)
        other_ref[...] = jnp.zeros_like(other_ref)

        @pl.loop(0, blocks)
        def _(k):
            slot = slots_ref[k]
            relative = (slot & (row_count - 1)) ^ row_ref[0]
            place = (relative >> 1 & 1) * depth + (relative >> 2)
            place = place + (slot - (slot & (row_count - 1))) // 2

            @pl.when(relative & 1 == 0)
            def _():
                own_ref[place] = tiles_ref[k]

            @pl.when(relative & 1 == 1)
            def _():
                other_ref[place] = tiles_ref[k]

    shape = jax.ShapeDtypeStruct((col_count * row_count // 2, side, side), tiles.dtype)
    smem = pl.BlockSpec(memory_space=pltpu.SMEM)
    vmem = pl.BlockSpec(memory_space=pltpu.VMEM)
    return pl.pallas_call(
        body,
        out_shape=(shape, shape),
        in_specs=[smem, smem, vmem] + [pl.BlockSpec(memory_space=pl.ANY)] * len(later_than),
        out_specs=(vmem, vmem),
        compiler_params=pltpu.CompilerParams(vmem_limit_bytes=(2 * (blocks + row_count * col_count) * side * side * 2) + (1 << 20)),
        cost_estimate=pl.CostEstimate(flops=flops, bytes_accessed=10**6, transcendentals=0),
    )(slots, row.reshape(1), tiles, *later_than)


def rounded(x):
    return lax.optimization_barrier(x.astype(jnp.bfloat16))


def local(features, weight, grad_out, tiles, slots):
    tile_blocks = tiles[0, 0]
    tile_slots = slots[0, 0]
    own_rows, width = features.shape
    side = tile_blocks.shape[1]
    row_count = lax.axis_size("row")
    col_count = lax.axis_size("col")
    row = lax.axis_index("row")
    col = lax.axis_index("col")
    core = row & 1
    depth = row_count // 4
    f32 = jnp.float32
    bf16 = jnp.bfloat16

    def direct(bit, low, high):
        return [swap(features, "row", 4 * k + bit) if k or bit else features for k in reversed(range(low, high))][::-1]

    straight = 1
    far = jnp.concatenate(direct(0, straight, depth))
    near = direct(0, 0, straight)
    near_x = jnp.concatenate(direct(2, 0, straight))
    panel = jnp.concatenate(near + [far])
    far_x = swap(far, "row", 2)

    cotangent = grad_out
    for bit in bits(col_count):
        got = swap(cotangent, "col", bit)
        low = jnp.where(col & bit == 0, cotangent, got)
        high = jnp.where(col & bit == 0, got, cotangent)
        cotangent = jnp.concatenate([low, high])
    own_tile, other_tile = dense_tile(tile_blocks, tile_slots, row, col, row_count, col_count, 3000000000, [far])
    own_tile = own_tile.reshape(col_count, 2, depth, side, side)
    other_tile = other_tile.reshape(col_count, 2, depth, side, side)

    def forward(quarter, block):
        return jnp.einsum(
            "bpij,pjf->bif",
            (own_tile if quarter < 2 else other_tile)[:, quarter % 2],
            block.reshape(depth, side, width),
            preferred_element_type=f32,
        )

    panel_c = swap(panel, "row", 1)
    partial = forward(0, panel) + forward(2, panel_c)
    far_x, cotangent, partial = lax.optimization_barrier((far_x, cotangent, partial))
    panel_x = jnp.concatenate([near_x, far_x])
    partial = partial + forward(1, panel_x) + forward(3, swap(panel_x, "row", 1))
    for bit in bits(col_count):
        sent, other_tile = lax.optimization_barrier((partial.astype(bf16), other_tile))
        got = swap(sent, "col", bit)
        partial = sent.astype(f32) + got.astype(f32)
    partner = swap(other_tile, "row", 1)
    aggregated = partial.astype(bf16).reshape(-1, width)
    pre = jnp.dot(aggregated, weight, preferred_element_type=f32)
    sigmoid_pre = jax.nn.sigmoid(pre)
    grad_pre = (
        cotangent.astype(f32) * sigmoid_pre * (1.0 + pre * (1.0 - sigmoid_pre))
    ).astype(bf16)
    partner_grad_pre = swap(grad_pre, "row", 1)
    partner_aggregated = swap(aggregated, "row", 1)

    def panel_of(rows):
        grad_agg = jnp.dot(rows, weight.T, preferred_element_type=f32).astype(bf16)
        return grad_agg.reshape(col_count, side, width)

    row_panel = panel_of(grad_pre)
    partner_panel = panel_of(partner_grad_pre)

    def backward(quarter):
        spec = "bpij,bif->pjf"
        own = jnp.einsum(spec, own_tile[:, quarter], row_panel, preferred_element_type=f32)
        return own + jnp.einsum(spec, partner[:, quarter], partner_panel, preferred_element_type=f32)

    sent_x = backward(1).astype(bf16)
    sent_x, pre = lax.optimization_barrier((sent_x, pre))
    got_x = swap(sent_x, "row", 2)
    mine = backward(0)

    columns = [
        lax.dynamic_slice_in_dim(rows, core * (width // 2), width // 2, 1)
        for rows in (aggregated, partner_aggregated)
    ]
    half = jnp.dot(columns[0].T, grad_pre, preferred_element_type=f32)
    half = half + jnp.dot(columns[1].T, partner_grad_pre, preferred_element_type=f32)
    half = total([half], bf16, 3000000000, [sent_x])

    mine = mine + got_x.astype(f32)
    sent_z = [mine[k].astype(bf16) for k in range(1, depth)]
    half = total([half] + [swap(half, "row", 4 * k) for k in range(1, depth)], bf16, 3 * 10**9, [sent_z[-1]])
    for k in (1,):
        sent_z[k - 1] = total([sent_z[k - 1]], bf16, 100000000, [half])
    got_z = [swap(sent_z[k - 1], "row", 4 * k) for k in range(1, depth)]
    half = total([half], bf16, 5 * 10**9)
    half = total([half, swap(half, "row", 2)], f32, 10**8)
    total_nodes = own_rows * row_count * col_count
    scale = 1.0 / math.sqrt(total_nodes)
    grad_sum = total([mine[0]] + got_z, f32, 3 * 10**9)
    grad_in, grad_weight = finish([grad_sum], half, swap(half, "row", 1), core, scale)

    start = col * own_rows
    own_pre = lax.dynamic_slice_in_dim(pre, start, own_rows)
    own_sigmoid = lax.dynamic_slice_in_dim(sigmoid_pre, start, own_rows)
    activated = (own_pre * own_sigmoid).astype(bf16)
    return (activated, grad_weight, grad_in)


def solution(mesh):
    in_specs = (
        P(("row", "col"), None),
        P(),
        P(("row", "col"), None),
        P("row", "col", None, None, None),
        P("row", "col", None),
    )
    out_specs = (P(("row", "col"), None), P(), P(("row", "col"), None))
    return jax.shard_map(local, mesh=mesh, in_specs=in_specs, out_specs=out_specs, check_vma=False)
```

```python
import math

import jax
import jax.numpy as jnp
from jax import lax
from jax.experimental import pallas as pl
from jax.experimental.pallas import tpu as pltpu
from jax.sharding import PartitionSpec as P


def swap(x, axis, bit):
    return lax.ppermute(x, axis, [(i, i ^ bit) for i in range(lax.axis_size(axis))])


def bits(count):
    return [1 << k for k in range(count.bit_length() - 1)]


def total(terms, dtype, flops, later_than=()):
    count = len(terms)

    def body(*refs):
        values = [ref[...].astype(jnp.float32) for ref in refs[:count]]
        while len(values) > 1:
            values = [a + b for a, b in zip(values[::2], values[1::2])]
        refs[-1][...] = values[0].astype(dtype)

    shape = jax.ShapeDtypeStruct(terms[0].shape, dtype)
    in_specs = [pl.BlockSpec(memory_space=pltpu.VMEM)] * count
    in_specs += [pl.BlockSpec(memory_space=pl.ANY)] * len(later_than)
    return pl.pallas_call(
        body,
        out_shape=shape,
        in_specs=in_specs,
        out_specs=pl.BlockSpec(memory_space=pltpu.VMEM),
        compiler_params=pltpu.CompilerParams(vmem_limit_bytes=4 << 20),
        cost_estimate=pl.CostEstimate(flops=flops, bytes_accessed=4 * shape.size, transcendentals=0),
    )(*terms, *later_than)


def tree_sum(terms):
    while len(terms) > 1:
        terms = [a + b for a, b in zip(terms[::2], terms[1::2])]
    return terms[0]


def finish(terms, half, other, core, scale):
    count = len(terms)
    rows, width = half.shape

    def body(core_ref, *refs):
        half_ref, other_ref, grad_ref, weight_ref = refs[count:]
        value = refs[0][...]
        for ref in refs[1:count]:
            value = value + ref[...].astype(jnp.float32)
        grad_ref[...] = value.astype(jnp.bfloat16)
        first = pl.multiple_of(core_ref[0] * rows, rows)
        second = pl.multiple_of(rows - core_ref[0] * rows, rows)
        weight_ref[pl.ds(first, rows), :] = half_ref[...] * scale
        weight_ref[pl.ds(second, rows), :] = other_ref[...] * scale

    vmem = pl.BlockSpec(memory_space=pltpu.VMEM)
    return pl.pallas_call(
        body,
        out_shape=(
            jax.ShapeDtypeStruct(terms[0].shape, jnp.bfloat16),
            jax.ShapeDtypeStruct((2 * rows, width), jnp.float32),
        ),
        in_specs=[pl.BlockSpec(memory_space=pltpu.SMEM)] + [vmem] * (count + 2),
        out_specs=(vmem, vmem),
        compiler_params=pltpu.CompilerParams(vmem_limit_bytes=4 << 20),
        cost_estimate=pl.CostEstimate(flops=10**6, bytes_accessed=10**6, transcendentals=0),
    )(core.reshape(1), *terms, half, other)


def dense_tile(tiles, slots, row, col, row_count, col_count, flops, later_than):
    blocks, side, _ = tiles.shape
    depth = row_count // 4

    def body(slots_ref, row_ref, tiles_ref, *refs):
        own_ref, other_ref = refs[-2:]
        own_ref[...] = jnp.zeros_like(own_ref)
        other_ref[...] = jnp.zeros_like(other_ref)

        @pl.loop(0, blocks)
        def _(k):
            slot = slots_ref[k]
            relative = (slot & (row_count - 1)) ^ row_ref[0]
            place = (relative >> 1 & 1) * depth + (relative >> 2)
            place = place + (slot - (slot & (row_count - 1))) // 2

            @pl.when(relative & 1 == 0)
            def _():
                own_ref[place] = tiles_ref[k]

            @pl.when(relative & 1 == 1)
            def _():
                other_ref[place] = tiles_ref[k]

    shape = jax.ShapeDtypeStruct((col_count * row_count // 2, side, side), tiles.dtype)
    smem = pl.BlockSpec(memory_space=pltpu.SMEM)
    vmem = pl.BlockSpec(memory_space=pltpu.VMEM)
    return pl.pallas_call(
        body,
        out_shape=(shape, shape),
        in_specs=[smem, smem, vmem] + [pl.BlockSpec(memory_space=pl.ANY)] * len(later_than),
        out_specs=(vmem, vmem),
        compiler_params=pltpu.CompilerParams(vmem_limit_bytes=(2 * (blocks + row_count * col_count) * side * side * 2) + (1 << 20)),
        cost_estimate=pl.CostEstimate(flops=flops, bytes_accessed=10**6, transcendentals=0),
    )(slots, row.reshape(1), tiles, *later_than)


def rounded(x):
    return lax.optimization_barrier(x.astype(jnp.bfloat16))


def local(features, weight, grad_out, tiles, slots):
    tile_blocks = tiles[0, 0]
    tile_slots = slots[0, 0]
    own_rows, width = features.shape
    side = tile_blocks.shape[1]
    row_count = lax.axis_size("row")
    col_count = lax.axis_size("col")
    row = lax.axis_index("row")
    col = lax.axis_index("col")
    core = row & 1
    depth = row_count // 4
    f32 = jnp.float32
    bf16 = jnp.bfloat16

    def direct(bit, low, high):
        return [swap(features, "row", 4 * k + bit) if k or bit else features for k in reversed(range(low, high))][::-1]

    straight = 1
    far = jnp.concatenate(direct(0, straight, depth))
    near = direct(0, 0, straight)
    near_x = jnp.concatenate(direct(2, 0, straight))
    panel = jnp.concatenate(near + [far])
    far_x = swap(far, "row", 2)

    cotangent = grad_out
    for bit in bits(col_count):
        got = swap(cotangent, "col", bit)
        low = jnp.where(col & bit == 0, cotangent, got)
        high = jnp.where(col & bit == 0, got, cotangent)
        cotangent = jnp.concatenate([low, high])
    own_tile, other_tile = dense_tile(tile_blocks, tile_slots, row, col, row_count, col_count, 3000000000, [far])
    own_tile = own_tile.reshape(col_count, 2, depth, side, side)
    other_tile = other_tile.reshape(col_count, 2, depth, side, side)

    def forward(quarter, block):
        return jnp.einsum(
            "bpij,pjf->bif",
            (own_tile if quarter < 2 else other_tile)[:, quarter % 2],
            block.reshape(depth, side, width),
            preferred_element_type=f32,
        )

    panel_c = swap(panel, "row", 1)
    partial = forward(0, panel) + forward(2, panel_c)
    far_x, cotangent, partial = lax.optimization_barrier((far_x, cotangent, partial))
    panel_x = jnp.concatenate([near_x, far_x])
    partial = partial + forward(1, panel_x) + forward(3, swap(panel_x, "row", 1))
    for bit in bits(col_count):
        sent, other_tile = lax.optimization_barrier((partial.astype(bf16), other_tile))
        got = swap(sent, "col", bit)
        partial = sent.astype(f32) + got.astype(f32)
    partner = swap(other_tile, "row", 1)
    aggregated = partial.astype(bf16).reshape(-1, width)
    pre = jnp.dot(aggregated, weight, preferred_element_type=f32)
    sigmoid_pre = jax.nn.sigmoid(pre)
    grad_pre = (
        cotangent.astype(f32) * sigmoid_pre * (1.0 + pre * (1.0 - sigmoid_pre))
    ).astype(bf16)
    partner_grad_pre = swap(grad_pre, "row", 1)
    partner_aggregated = swap(aggregated, "row", 1)

    def panel_of(rows):
        grad_agg = jnp.dot(rows, weight.T, preferred_element_type=f32).astype(bf16)
        return grad_agg.reshape(col_count, side, width)

    row_panel = panel_of(grad_pre)
    partner_panel = panel_of(partner_grad_pre)

    def backward(quarter):
        spec = "bpij,bif->pjf"
        own = jnp.einsum(spec, own_tile[:, quarter], row_panel, preferred_element_type=f32)
        return own + jnp.einsum(spec, partner[:, quarter], partner_panel, preferred_element_type=f32)

    sent_x = backward(1).astype(bf16)
    got_x = swap(sent_x, "row", 2)
    mine = backward(0)

    columns = [
        lax.dynamic_slice_in_dim(rows, core * (width // 2), width // 2, 1)
        for rows in (aggregated, partner_aggregated)
    ]
    half = jnp.dot(columns[0].T, grad_pre, preferred_element_type=f32)
    half = half + jnp.dot(columns[1].T, partner_grad_pre, preferred_element_type=f32)
    half = total([half], bf16, 3000000000, [sent_x])

    mine = mine + got_x.astype(f32)
    sent_z = [mine[k].astype(bf16) for k in range(1, depth)]
    half = total([half] + [swap(half, "row", 4 * k) for k in range(1, depth)], bf16, 3 * 10**9, [sent_z[-1]])
    for k in (1,):
        sent_z[k - 1] = total([sent_z[k - 1]], bf16, 100000000, [half])
    got_z = [swap(sent_z[k - 1], "row", 4 * k) for k in range(1, depth)]
    half = total([half], bf16, 5 * 10**9)
    half = total([half, swap(half, "row", 2)], f32, 10**8)
    total_nodes = own_rows * row_count * col_count
    scale = 1.0 / math.sqrt(total_nodes)
    grad_sum = total([mine[0]] + got_z, f32, 3 * 10**9)
    grad_in, grad_weight = finish([grad_sum], half, swap(half, "row", 1), core, scale)

    start = col * own_rows
    own_pre = lax.dynamic_slice_in_dim(pre, start, own_rows)
    own_sigmoid = lax.dynamic_slice_in_dim(sigmoid_pre, start, own_rows)
    activated = (own_pre * own_sigmoid).astype(bf16)
    return (activated, grad_weight, grad_in)


def solution(mesh):
    in_specs = (
        P(("row", "col"), None),
        P(),
        P(("row", "col"), None),
        P("row", "col", None, None, None),
        P("row", "col", None),
    )
    out_specs = (P(("row", "col"), None), P(), P(("row", "col"), None))
    return jax.shard_map(local, mesh=mesh, in_specs=in_specs, out_specs=out_specs, check_vma=False)
```

```python
import math

import jax
import jax.numpy as jnp
from jax import lax
from jax.experimental import pallas as pl
from jax.experimental.pallas import tpu as pltpu
from jax.sharding import PartitionSpec as P


def swap(x, axis, bit):
    return lax.ppermute(x, axis, [(i, i ^ bit) for i in range(lax.axis_size(axis))])


def bits(count):
    return [1 << k for k in range(count.bit_length() - 1)]


def total(terms, dtype, flops, later_than=()):
    count = len(terms)

    def body(*refs):
        values = [ref[...].astype(jnp.float32) for ref in refs[:count]]
        while len(values) > 1:
            values = [a + b for a, b in zip(values[::2], values[1::2])]
        refs[-1][...] = values[0].astype(dtype)

    shape = jax.ShapeDtypeStruct(terms[0].shape, dtype)
    in_specs = [pl.BlockSpec(memory_space=pltpu.VMEM)] * count
    in_specs += [pl.BlockSpec(memory_space=pl.ANY)] * len(later_than)
    return pl.pallas_call(
        body,
        out_shape=shape,
        in_specs=in_specs,
        out_specs=pl.BlockSpec(memory_space=pltpu.VMEM),
        compiler_params=pltpu.CompilerParams(vmem_limit_bytes=4 << 20),
        cost_estimate=pl.CostEstimate(flops=flops, bytes_accessed=4 * shape.size, transcendentals=0),
    )(*terms, *later_than)


def tree_sum(terms):
    while len(terms) > 1:
        terms = [a + b for a, b in zip(terms[::2], terms[1::2])]
    return terms[0]


def finish(terms, half, other, core, scale):
    count = len(terms)
    rows, width = half.shape

    def body(core_ref, *refs):
        half_ref, other_ref, grad_ref, weight_ref = refs[count:]
        value = refs[0][...]
        for ref in refs[1:count]:
            value = value + ref[...].astype(jnp.float32)
        grad_ref[...] = value.astype(jnp.bfloat16)
        first = pl.multiple_of(core_ref[0] * rows, rows)
        second = pl.multiple_of(rows - core_ref[0] * rows, rows)
        weight_ref[pl.ds(first, rows), :] = half_ref[...] * scale
        weight_ref[pl.ds(second, rows), :] = other_ref[...] * scale

    vmem = pl.BlockSpec(memory_space=pltpu.VMEM)
    return pl.pallas_call(
        body,
        out_shape=(
            jax.ShapeDtypeStruct(terms[0].shape, jnp.bfloat16),
            jax.ShapeDtypeStruct((2 * rows, width), jnp.float32),
        ),
        in_specs=[pl.BlockSpec(memory_space=pltpu.SMEM)] + [vmem] * (count + 2),
        out_specs=(vmem, vmem),
        compiler_params=pltpu.CompilerParams(vmem_limit_bytes=4 << 20),
        cost_estimate=pl.CostEstimate(flops=10**6, bytes_accessed=10**6, transcendentals=0),
    )(core.reshape(1), *terms, half, other)


def dense_tile(tiles, slots, row, col, row_count, col_count, flops, later_than):
    blocks, side, _ = tiles.shape
    depth = row_count // 4

    def body(slots_ref, row_ref, tiles_ref, *refs):
        own_ref, other_ref = refs[-2:]
        own_ref[...] = jnp.zeros_like(own_ref)
        other_ref[...] = jnp.zeros_like(other_ref)

        @pl.loop(0, blocks)
        def _(k):
            slot = slots_ref[k]
            relative = (slot & (row_count - 1)) ^ row_ref[0]
            place = (relative >> 1 & 1) * depth + (relative >> 2)
            place = place + (slot - (slot & (row_count - 1))) // 2

            @pl.when(relative & 1 == 0)
            def _():
                own_ref[place] = tiles_ref[k]

            @pl.when(relative & 1 == 1)
            def _():
                other_ref[place] = tiles_ref[k]

    shape = jax.ShapeDtypeStruct((col_count * row_count // 2, side, side), tiles.dtype)
    smem = pl.BlockSpec(memory_space=pltpu.SMEM)
    vmem = pl.BlockSpec(memory_space=pltpu.VMEM)
    return pl.pallas_call(
        body,
        out_shape=(shape, shape),
        in_specs=[smem, smem, vmem] + [pl.BlockSpec(memory_space=pl.ANY)] * len(later_than),
        out_specs=(vmem, vmem),
        compiler_params=pltpu.CompilerParams(vmem_limit_bytes=(2 * (blocks + row_count * col_count) * side * side * 2) + (1 << 20)),
        cost_estimate=pl.CostEstimate(flops=flops, bytes_accessed=10**6, transcendentals=0),
    )(slots, row.reshape(1), tiles, *later_than)


def rounded(x):
    return lax.optimization_barrier(x.astype(jnp.bfloat16))


def local(features, weight, grad_out, tiles, slots):
    tile_blocks = tiles[0, 0]
    tile_slots = slots[0, 0]
    own_rows, width = features.shape
    side = tile_blocks.shape[1]
    row_count = lax.axis_size("row")
    col_count = lax.axis_size("col")
    row = lax.axis_index("row")
    col = lax.axis_index("col")
    core = row & 1
    depth = row_count // 4
    f32 = jnp.float32
    bf16 = jnp.bfloat16

    def direct(bit, low, high):
        return [swap(features, "row", 4 * k + bit) if k or bit else features for k in reversed(range(low, high))][::-1]

    straight = 1
    pieces = direct(0, straight, depth)
    far = jnp.concatenate(pieces)
    near = direct(0, 0, straight)
    near_x = jnp.concatenate(direct(2, 0, straight))
    panel = jnp.concatenate(near + pieces)
    far_x = swap(far, "row", 2)

    cotangent = grad_out
    for bit in bits(col_count):
        got = swap(cotangent, "col", bit)
        low = jnp.where(col & bit == 0, cotangent, got)
        high = jnp.where(col & bit == 0, got, cotangent)
        cotangent = jnp.concatenate([low, high])
    own_tile, other_tile = dense_tile(tile_blocks, tile_slots, row, col, row_count, col_count, 3000000000, [far])
    own_tile = own_tile.reshape(col_count, 2, depth, side, side)
    other_tile = other_tile.reshape(col_count, 2, depth, side, side)

    def forward(quarter, block):
        return jnp.einsum(
            "bpij,pjf->bif",
            (own_tile if quarter < 2 else other_tile)[:, quarter % 2],
            block.reshape(depth, side, width),
            preferred_element_type=f32,
        )

    panel_c = swap(panel, "row", 1)
    partial = forward(0, panel) + forward(2, panel_c)
    far_x, cotangent, partial = lax.optimization_barrier((far_x, cotangent, partial))
    panel_x = jnp.concatenate([near_x, far_x])
    partial = partial + forward(1, panel_x) + forward(3, swap(panel_x, "row", 1))
    for bit in bits(col_count):
        sent, other_tile = lax.optimization_barrier((partial.astype(bf16), other_tile))
        got = swap(sent, "col", bit)
        partial = sent.astype(f32) + got.astype(f32)
    partner = swap(other_tile, "row", 1)
    aggregated = partial.astype(bf16).reshape(-1, width)
    pre = jnp.dot(aggregated, weight, preferred_element_type=f32)
    sigmoid_pre = jax.nn.sigmoid(pre)
    grad_pre = (
        cotangent.astype(f32) * sigmoid_pre * (1.0 + pre * (1.0 - sigmoid_pre))
    ).astype(bf16)
    partner_grad_pre = swap(grad_pre, "row", 1)
    partner_aggregated = swap(aggregated, "row", 1)

    def panel_of(rows):
        grad_agg = jnp.dot(rows, weight.T, preferred_element_type=f32).astype(bf16)
        return grad_agg.reshape(col_count, side, width)

    row_panel = panel_of(grad_pre)
    partner_panel = panel_of(partner_grad_pre)

    def backward(quarter):
        spec = "bpij,bif->pjf"
        own = jnp.einsum(spec, own_tile[:, quarter], row_panel, preferred_element_type=f32)
        return own + jnp.einsum(spec, partner[:, quarter], partner_panel, preferred_element_type=f32)

    sent_x = backward(1).astype(bf16)
    sent_x, pre = lax.optimization_barrier((sent_x, pre))
    got_x = swap(sent_x, "row", 2)
    mine = backward(0)

    columns = [
        lax.dynamic_slice_in_dim(rows, core * (width // 2), width // 2, 1)
        for rows in (aggregated, partner_aggregated)
    ]
    half = jnp.dot(columns[0].T, grad_pre, preferred_element_type=f32)
    half = half + jnp.dot(columns[1].T, partner_grad_pre, preferred_element_type=f32)
    half = total([half], bf16, 3000000000, [sent_x])

    mine = mine + got_x.astype(f32)
    sent_z = [mine[k].astype(bf16) for k in range(1, depth)]
    half = total([half] + [swap(half, "row", 4 * k) for k in range(1, depth)], bf16, 3 * 10**9, [sent_z[-1]])
    for k in (1,):
        sent_z[k - 1] = total([sent_z[k - 1]], bf16, 100000000, [half])
    got_z = [swap(sent_z[k - 1], "row", 4 * k) for k in range(1, depth)]
    half = total([half], bf16, 5 * 10**9)
    half = total([half, swap(half, "row", 2)], f32, 10**8)
    total_nodes = own_rows * row_count * col_count
    scale = 1.0 / math.sqrt(total_nodes)
    grad_sum = total([mine[0]] + got_z, f32, 3 * 10**9)
    grad_in, grad_weight = finish([grad_sum], half, swap(half, "row", 1), core, scale)

    start = col * own_rows
    own_pre = lax.dynamic_slice_in_dim(pre, start, own_rows)
    own_sigmoid = lax.dynamic_slice_in_dim(sigmoid_pre, start, own_rows)
    activated = (own_pre * own_sigmoid).astype(bf16)
    return (activated, grad_weight, grad_in)


def solution(mesh):
    in_specs = (
        P(("row", "col"), None),
        P(),
        P(("row", "col"), None),
        P("row", "col", None, None, None),
        P("row", "col", None),
    )
    out_specs = (P(("row", "col"), None), P(), P(("row", "col"), None))
    return jax.shard_map(local, mesh=mesh, in_specs=in_specs, out_specs=out_specs, check_vma=False)
```
